32 devices in a mesh: mem: 4 (over y, x), cell: 8 (over z, core).
Axes of the slice: x: 2, y: 2, z: 4, core: 2. Of those that a mesh axis runs over, the one named last changes fastest.
Arguments:
- depth: float32 [64, 131072], P('mem', 'cell'), may hold values from 1 to 3
- discharge: float32 [64, 131072], P('mem', 'cell'), may hold values from -1.5 to 1.5
- gate: int32 [131072], P('cell'), may hold values from 0 to 1, as said below
- pump: int32 [2, 131072], P(None, 'cell'), may hold values 0 or 1
- pump_rate: float32 [131072], P('cell'), may hold values from 1 to 5
- obs_index: int32 [8, 512], P('cell'), may hold values from 0 to 16383, as said below
- obs_value: float32 [8, 512], P('cell'), may hold values from 1 to 3
- obs_error: float32 [8, 512], P('cell'), may hold values from 0.25 to 1.04
Outputs:
- depth_analysis: float32 [64, 131072], P('mem', 'cell')
- discharge_analysis: float32 [64, 131072], P('mem', 'cell')
The draws below stay inside these ranges and needn't reach their ends.
Inputs may be any that keep to these rules, and one draw needn't show every extreme that they name: The gate on the first face of every slab after the first (cells s * 16384 with s >= 1) is open. `obs_index`: the offsets of one slab are distinct.
All inputs are finite; a program needn't handle non-finite values. No bound on the sum of `pump` on one device may be relied on, other than what follows from the above.
Results may differ from the reference program's by a relative error of at most 0.0003.
Values sent between devices are 32-bit elements; how exact they have to be, the bound alone decides.
A program may use at most 64 MiB of HBM per device.

```python
import math
import jax
import jax.numpy as jnp
from jax import lax

MEMBERS = 64
CELL_DEV = 16384
PER = 512
STEPS = 2
NS_ITERS = 12
SLABS = 8
OBS_SLAB = 512
CELLS = 131072
UNITS = 256
NOBS = 4096


def draw_gate(key, part):
    opened = jax.random.randint(jax.random.fold_in(key, 41), (SLABS, CELL_DEV), 0, 4) > 0
    values = opened.astype(jnp.int32)
    values = values.at[:, 0].set(1)
    return values.reshape(-1).astype(jnp.int32)


def draw_obs_index(key, part):
    keys = jax.random.split(jax.random.fold_in(key, 23), SLABS)
    perms = jax.vmap(lambda single: jax.random.permutation(single, CELL_DEV))(keys)
    return perms[:, :OBS_SLAB].astype(jnp.int32)


def draw_obs_error(key, part):
    shape = (SLABS, OBS_SLAB)
    slab_pos = jnp.arange(SLABS, dtype=jnp.float32)[:, None] / max(SLABS - 1, 1)
    growth = jnp.sqrt(1.0 + 2.0 * slab_pos)
    base = jnp.exp(jax.random.uniform(jax.random.fold_in(key, 31), shape, jnp.float32, jnp.log(0.25), jnp.log(0.6)))
    return base * growth


def set_ends(drawn, rng, least, high):
    shape = drawn.shape
    place = [jax.random.randint(jax.random.fold_in(rng, axis), (), 0, shape[axis]) for axis in range(len(shape))]
    drawn = drawn.at[tuple(place)].set(least)
    longest = shape.index(max(shape))
    place[longest] = (place[longest] + 1) % shape[longest]
    return drawn.at[tuple(place)].set(high)


def levels(key, shape, shards, smallest, top_value):
    def one(dim, blocks):
        heights = jax.random.uniform(jax.random.fold_in(jax.random.fold_in(key, 6), dim), (blocks,), jnp.float32, smallest / len(shards), top_value / len(shards))
        return jnp.repeat(jnp.exp(heights), shape[dim] // blocks).reshape((-1,) + (1,) * (len(shape) - dim - 1))

    gain = one(*shards[0])
    for cut in shards[1:]:
        gain = gain * one(*cut)
    return gain


def scatter_about(stream_key, dims, deviation, reach, cuts=(), kind=jnp.bfloat16):
    array = deviation * jax.random.normal(stream_key, dims, jnp.float32)
    if cuts:
        array = array * levels(stream_key, dims, cuts, -0.22, 0.18)
    return jnp.clip(array, -reach, reach).astype(kind)


def setup_inputs(seed: int = 0) -> dict:
    key_list = jax.random.split(jax.random.key(seed), 9)
    return {
        "depth": jnp.clip(1.0 + 2.0 * jax.random.uniform(key_list[0], (MEMBERS, CELLS), jnp.float32) ** levels(key_list[0], (MEMBERS, CELLS), ((0, 4), (1, 8)), -0.2, 0.2), 1.0, 3.0),
        "discharge": scatter_about(key_list[1], (MEMBERS, CELLS), 0.4, 1.5, ((0, 4), (1, 8)), jnp.float32),
        "gate": draw_gate(jax.random.fold_in(key_list[8], 71), 0),
        "pump": set_ends((jax.random.randint(key_list[3], (STEPS, CELLS), 0, 4) < 1).astype(jnp.int32), jax.random.fold_in(key_list[3], 1), 0, 1),
        "pump_rate": jnp.clip(jnp.exp(math.log(5.0) - 1.609438 * jax.random.uniform(key_list[4], (CELLS,), jnp.float32) ** levels(key_list[4], (CELLS,), ((0, 8),), -0.2, 0.2)), 1.0, 5.0),
        "obs_index": draw_obs_index(jax.random.fold_in(key_list[8], 71), 0),
        "obs_value": jnp.clip(1.0 + 2.0 * jax.random.uniform(key_list[6], (SLABS, OBS_SLAB), jnp.float32) ** levels(key_list[6], (SLABS, OBS_SLAB), ((0, 8),), -0.2, 0.2), 1.0, 3.0),
        "obs_error": draw_obs_error(jax.random.fold_in(key_list[8], 71), 0),
    }


gravity = 9.81
step_dt = 0.06

def face_fluxes(depth_left, flow_left, depth_right, flow_right, faces):
    opened = faces > 0.5
    safe_dl = jnp.where(opened, depth_left, 1.0)
    safe_fl = jnp.where(opened, flow_left, 0.0)
    safe_dr = jnp.where(opened, depth_right, 1.0)
    safe_fr = jnp.where(opened, flow_right, 0.0)
    speed_left = safe_fl / safe_dl
    speed_right = safe_fr / safe_dr
    wave_left = jnp.sqrt(gravity * safe_dl)
    wave_right = jnp.sqrt(gravity * safe_dr)
    slowest = jnp.minimum(jnp.minimum(speed_left - wave_left, speed_right - wave_right), 0.0)
    fastest = jnp.maximum(jnp.maximum(speed_left + wave_left, speed_right + wave_right), 0.0)
    moment_left = safe_fl * speed_left + 0.5 * gravity * safe_dl * safe_dl
    moment_right = safe_fr * speed_right + 0.5 * gravity * safe_dr * safe_dr
    spread = fastest - slowest
    mass = (fastest * safe_fl - slowest * safe_fr + slowest * fastest * (safe_dr - safe_dl)) / spread
    moment = (fastest * moment_left - slowest * moment_right + slowest * fastest * (safe_fr - safe_fl)) / spread
    mass = jnp.where(opened, mass, 0.0)
    left_side = jnp.where(opened, moment, 0.5 * gravity * depth_left * depth_left)
    right_side = jnp.where(opened, moment, 0.5 * gravity * depth_right * depth_right)
    return (mass, left_side, right_side)

def advance(depth_pad, flow_pad, faces, inflow):
    mass, left_side, right_side = face_fluxes(depth_pad[..., :-1], flow_pad[..., :-1], depth_pad[..., 1:], flow_pad[..., 1:], faces)
    depth_new = depth_pad[..., 1:-1] - step_dt * (mass[..., 1:] - mass[..., :-1]) + step_dt * inflow
    flow_new = flow_pad[..., 1:-1] - step_dt * (left_side[..., 1:] - right_side[..., :-1])
    return (depth_new, flow_new)

def batch_product(first, second):
    return jnp.einsum('uij,ujk->uik', first, second, precision=lax.Precision.HIGHEST)

def transform_units(grams, cross, factor_rho):
    count = grams.shape[-1]
    identity = jnp.eye(count, dtype=jnp.float32)
    system = identity + factor_rho * factor_rho / (count - 1) * grams
    norm_scale = jnp.sqrt(lax.optimization_barrier(jnp.sum(system * system, axis=(1, 2))))
    iterate = system / norm_scale[:, None, None]
    inverse = jnp.broadcast_to(identity, system.shape)

    def newton_step(turn, carry):
        current, invroot = carry
        factor = 1.5 * identity - 0.5 * batch_product(invroot, current)
        return (batch_product(current, factor), batch_product(factor, invroot))
    iterate, inverse = lax.fori_loop(0, NS_ITERS, newton_step, (iterate, inverse))
    root_weight = inverse / jnp.sqrt(norm_scale)[:, None, None]
    solved = batch_product(inverse, inverse) / norm_scale[:, None, None]
    mean_weight = factor_rho / (count - 1) * jnp.einsum('uij,uj->ui', solved, cross, precision=lax.Precision.HIGHEST)
    return factor_rho * (root_weight + mean_weight[:, :, None])

def reference(depth, discharge, gate, pump, pump_rate, obs_index, obs_value, obs_error):
    inner = gate[1:].astype(jnp.float32)
    faces = jnp.concatenate([jnp.zeros((1,), jnp.float32), inner, jnp.zeros((1,), jnp.float32)])

    def member_run(pair):
        depth_row, flow_row = pair
        for step in range(STEPS):
            inflow = pump_rate * pump[step].astype(jnp.float32)
            depth_row, flow_row = advance(jnp.pad(depth_row, 1), jnp.pad(flow_row, 1), faces, inflow)
        return (depth_row, flow_row)
    depth_fc, flow_fc = lax.map(member_run, (depth, discharge))
    count = depth_fc.shape[0]
    observed = ((jnp.arange(SLABS, dtype=jnp.int32) * CELL_DEV)[:, None] + obs_index).reshape(-1).astype(jnp.int32)
    home = (observed // PER).astype(jnp.int32)
    seen = depth_fc[:, observed]
    seen_mean = lax.optimization_barrier(jnp.mean(seen, axis=0))
    precision_obs = 1.0 / obs_error.reshape(-1)
    scaled = (seen - seen_mean[None, :]) * precision_obs[None, :]
    innov = (obs_value.reshape(-1) - seen_mean) * precision_obs
    total_misfit = jnp.sum(innov * innov)
    total_spread = jnp.sum(scaled * scaled) / (count - 1)
    factor_rho = jnp.sqrt(total_misfit / (total_spread + NOBS))

    def add_slab(carry, slab):
        grams, cross = carry
        block = lax.dynamic_slice_in_dim(scaled, slab * OBS_SLAB, OBS_SLAB, 1)
        innov_block = lax.dynamic_slice_in_dim(innov, slab * OBS_SLAB, OBS_SLAB, 0)
        homes = lax.dynamic_slice_in_dim(home, slab * OBS_SLAB, OBS_SLAB, 0)
        outer = jnp.einsum('ik,jk->kij', block, block, precision=lax.Precision.HIGHEST)
        cross_terms = (block * innov_block[None, :]).T
        for offset in (-1, 0, 1):
            target = homes + offset
            target = jnp.where((target >= 0) & (target < UNITS), target, UNITS).astype(jnp.int32)
            grams = grams + jax.ops.segment_sum(outer, target, num_segments=UNITS + 1)[:UNITS]
            cross = cross + jax.ops.segment_sum(cross_terms, target, num_segments=UNITS + 1)[:UNITS]
        return ((grams, cross), None)
    start = (jnp.zeros((UNITS, count, count), jnp.float32), jnp.zeros((UNITS, count), jnp.float32))
    (grams, cross), _ = lax.scan(add_slab, start, jnp.arange(SLABS, dtype=jnp.int32))
    mixing = transform_units(grams, cross, factor_rho)
    fields = jnp.stack([depth_fc, flow_fc]).reshape(2, count, UNITS, PER)
    field_mean = lax.optimization_barrier(jnp.mean(fields, axis=1, keepdims=True))
    analysed = field_mean + jnp.einsum('fiur,uij->fjur', fields - field_mean, mixing, precision=lax.Precision.HIGHEST)
    restored = analysed.reshape(2, count, CELLS)
    return (restored[0], restored[1])
```

```python
import functools

import jax
import jax.numpy as jnp
from jax import lax
from jax.experimental import pallas as pl
from jax.experimental.pallas import tpu as pltpu
from jax.sharding import PartitionSpec as P

PER = 512
NS_ITERS = 12
LANES = 128
CHUNK = 1024
GROUP = 4
MESH = pl.DeviceIdType.MESH

gravity = 9.81
step_dt = 0.06


def rolled(x, shift):
    return pltpu.roll(x, shift % x.shape[1], 1)


def advance(h, q, opened, inflow):
    u = q / h
    c = jnp.sqrt(gravity * h)
    low = u - c
    top = u + c
    still = (0.5 * gravity) * h * h
    moment = q * u + still
    h_left = rolled(h, 1)
    q_left = rolled(q, 1)
    still_left = rolled(still, 1)
    moment_left = rolled(moment, 1)
    a = jnp.minimum(jnp.minimum(rolled(low, 1), low), 0.0)
    b = jnp.maximum(jnp.maximum(rolled(top, 1), top), 0.0)
    inverse = 1.0 / (b - a)
    ab = a * b
    mass = (b * q_left - a * q + ab * (h - h_left)) * inverse
    flux = (b * moment_left - a * moment + ab * (q - q_left)) * inverse
    mass = jnp.where(opened, mass, 0.0)
    left_side = jnp.where(opened, flux, still_left)
    right_side = jnp.where(opened, flux, still)
    h_new = h - step_dt * (rolled(mass, -1) - mass) + step_dt * inflow
    q_new = q - step_dt * (rolled(left_side, -1) - right_side)
    return h_new, q_new


def split(x):
    high = x.astype(jnp.bfloat16)
    return high, (x - high.astype(jnp.float32)).astype(jnp.bfloat16)


def dot(x, y):
    return jnp.dot(x, y, preferred_element_type=jnp.float32)


def dot_t(x, y):
    return lax.dot_general(x, y, (((1,), (1,)), ((), ())), preferred_element_type=jnp.float32)


def kernel(
    quarters, slabs,
    depth, flow, gate, pump, rate, obs_index, obs_value, obs_error,
    out_depth, out_flow,
    d_pad, f_pad, g_pad, p_pad, r_pad, fc_d, fc_f, win_d, win_f, an_d, an_f,
    obs_rows, blocks, edge_src, stats, mem_stats, cell_src, cell_stats, mixing,
    load_sem, halo_send, halo_recv, go_send, go_recv, own_sem,
    edge_send, edge_recv, ms_send, ms_recv, cs_send, cs_recv, back_send, back_recv, back_own,
):
    me = lax.axis_index("mem")
    slab = lax.axis_index("cell")
    rows, cells = depth.shape
    members = rows * quarters
    quart = cells // quarters
    subs = quart // PER
    steps = pump.shape[0]
    total_obs = obs_index.shape[1] * slabs
    pads = (d_pad, f_pad, g_pad, p_pad, r_pad)
    sources = (depth, flow, gate, pump, rate)
    place = slab * quarters + me
    last_place = slabs * quarters - 1
    has_low = slab > 0
    has_high = slab < slabs - 1

    loads = [
        pltpu.make_async_copy(src, pad.at[:, pl.ds(LANES, cells)], load_sem.at[i])
        for i, (src, pad) in enumerate(zip(sources, pads))
    ]
    for copy in loads:
        copy.start()

    barrier = pltpu.get_barrier_semaphore()
    for k in range(1, quarters):
        pl.semaphore_signal(
            barrier, inc=1, device_id={"mem": (me + k) % quarters}, device_id_type=MESH
        )

    def greet(k, _):
        pl.semaphore_signal(barrier, inc=1, device_id={"cell": (slab + k) % slabs}, device_id_type=MESH)
        return 0

    for k in range(1, slabs):
        greet(k, 0)
    cross_low = jnp.logical_and(me == 0, has_low)
    cross_high = jnp.logical_and(me == quarters - 1, has_high)

    @pl.when(cross_low)
    def _():
        pl.semaphore_signal(
            barrier, inc=1, device_id={"mem": quarters - 1, "cell": (slab + slabs - 1) % slabs}, device_id_type=MESH
        )

    @pl.when(cross_high)
    def _():
        pl.semaphore_signal(
            barrier, inc=1, device_id={"mem": 0, "cell": (slab + 1) % slabs}, device_id_type=MESH
        )

    crossing = cross_low.astype(jnp.int32) + cross_high.astype(jnp.int32)
    pl.semaphore_wait(barrier, quarters - 1 + slabs - 1 + crossing)

    def halo(side, i):
        start = cells - LANES if side == 0 else 0
        target = 0 if side == 0 else cells + LANES
        return pltpu.make_async_remote_copy(
            src_ref=sources[i].at[:, pl.ds(start, LANES)],
            dst_ref=pads[i].at[:, pl.ds(target, LANES)],
            send_sem=halo_send.at[side, i],
            recv_sem=halo_recv.at[side, i],
            device_id={"cell": (slab + 1 if side == 0 else slab + slabs - 1) % slabs},
            device_id_type=MESH,
        )

    @pl.when(has_high)
    def _():
        for i in range(5):
            halo(0, i).start()

    @pl.when(has_low)
    def _():
        for i in range(5):
            halo(1, i).start()

    offsets = obs_index[...] - me * quart
    value = obs_value[...]
    precision = 1.0 / obs_error[...]
    coarse = offsets // LANES
    fine = offsets - coarse * LANES
    count = obs_index.shape[1]
    row_count = quart // LANES
    at_row = lax.broadcasted_iota(jnp.int32, (row_count, count), 0) == coarse
    at_lane = (lax.broadcasted_iota(jnp.int32, (LANES, count), 0) == fine).astype(jnp.float32)
    picked = jnp.concatenate(
        [jnp.where(at_row, value, 0.0), jnp.where(at_row, precision, 0.0)], axis=0
    )
    obs_rows[...] = lax.dot_general(
        picked, at_lane, (((1,), (1,)), ((), ())),
        precision=lax.Precision.HIGHEST, preferred_element_type=jnp.float32,
    )

    for copy in loads:
        copy.wait()

    @pl.when(has_low)
    def _():
        for i in range(5):
            halo(0, i).wait_recv()

    @pl.when(has_high)
    def _():
        for i in range(5):
            halo(1, i).wait_recv()

    width = CHUNK + 2 * LANES

    def forecast(chunk):
        start = pl.multiple_of(chunk * CHUNK, CHUNK)
        at = pl.ds(start, width)
        cell = lax.broadcasted_iota(jnp.int32, (1, width), 1) + (slab * cells + start - LANES)
        inside = jnp.logical_and(cell > 0, cell < slabs * cells)
        opened = jnp.logical_and(g_pad[:, at] > 0, inside)
        h = d_pad[:, at]
        q = f_pad[:, at]
        for step in range(steps):
            inflow = r_pad[:, at] * p_pad[step : step + 1, at].astype(jnp.float32)
            h, q = advance(h, q, opened, inflow)
        fc_d[:, pl.ds(start, CHUNK)] = h[:, LANES : LANES + CHUNK]
        fc_f[:, pl.ds(start, CHUNK)] = q[:, LANES : LANES + CHUNK]

    per_quart = quart // CHUNK

    def go(field, k, arriving=False):
        peer = (me + k) % quarters
        owner = (me - k + quarters) % quarters if arriving else me
        source = (fc_d, fc_f)[field]
        target = (win_d, win_f)[field]
        return pltpu.make_async_remote_copy(
            src_ref=source.at[:, pl.ds(pl.multiple_of(peer * quart, quart), quart)],
            dst_ref=target.at[pl.ds(pl.multiple_of(owner * rows, rows), rows), :],
            send_sem=go_send.at[field, k],
            recv_sem=go_recv.at[field, k],
            device_id={"mem": peer},
            device_id_type=MESH,
        )

    def keep(field):
        source = (fc_d, fc_f)[field]
        target = (win_d, win_f)[field]
        return pltpu.make_async_copy(
            source.at[:, pl.ds(pl.multiple_of(me * quart, quart), quart)],
            target.at[pl.ds(pl.multiple_of(me * rows, rows), rows), :],
            own_sem.at[field],
        )

    for k in range(1, quarters + 1):
        peer = (me + k) % quarters

        def one(j, _):
            forecast(peer * per_quart + j)
            return 0

        lax.fori_loop(0, per_quart, one, 0)
        if k < quarters:
            go(0, k).start()
        else:
            keep(0).start()
            keep(1).start()
    for k in range(1, quarters):
        go(1, k).start()

    keep(0).wait()
    keep(1).wait()
    for k in range(1, quarters):
        go(0, k, True).wait_recv()

    pieces = PER // LANES
    extra = 8
    first_extra = lax.broadcasted_iota(jnp.int32, (extra, PER), 0) == 0

    def obs_of(sub, base):
        first_row = base + sub * pieces
        at = [obs_rows[first_row + i : first_row + i + 1, :] for i in range(pieces)]
        return jnp.concatenate(at, axis=1)

    def gram(sub, total):
        x = win_d[:, sub * PER : (sub + 1) * PER]
        mean = jnp.mean(x, axis=0, keepdims=True)
        weight = obs_of(sub, row_count)
        scaled = (x - mean) * weight
        innov = (obs_of(sub, 0) - mean) * weight
        tall = jnp.concatenate(
            [
                scaled,
                jnp.where(first_extra, innov, 0.0),
                jnp.zeros((LANES - members - extra, PER), jnp.float32),
            ],
            axis=0,
        )
        high, low = split(tall)
        part = members + extra
        both = jnp.concatenate([high[:80], low[:80]], axis=0)
        first = dot_t(both, high)
        block = first[:part] + first[80 : 80 + part] + dot_t(high[:80], low)[:part]
        blocks[sub + 1] = block
        return total + block

    part = members + extra
    summed = jnp.zeros((part, LANES), jnp.float32)
    for sub in range(subs):
        summed = gram(sub, summed)
    ri = lax.broadcasted_iota(jnp.int32, (part, LANES), 0)
    ci = lax.broadcasted_iota(jnp.int32, (part, LANES), 1)
    diagonal = jnp.where(ri == ci, summed, 0.0)
    spread = jnp.sum(jnp.where(ri < members, diagonal, 0.0), keepdims=True)
    misfit = jnp.sum(jnp.where(ri == members, diagonal, 0.0), keepdims=True)
    lane = lax.broadcasted_iota(jnp.int32, (8, LANES), 1)
    mine = jnp.where(lane == 0, misfit, jnp.where(lane == 1, spread, 0.0))
    stats[...] = mine
    edge_src[0] = blocks[1]
    edge_src[1] = blocks[subs]

    def tell_mem(k):
        return pltpu.make_async_remote_copy(
            src_ref=stats, dst_ref=mem_stats.at[k],
            send_sem=ms_send.at[k], recv_sem=ms_recv.at[k],
            device_id={"mem": (me + k) % quarters}, device_id_type=MESH,
        )

    for k in range(1, quarters):
        tell_mem(k).start()

    def edge(side):
        other = (place + last_place if side == 0 else place + 1) % (last_place + 1)
        return pltpu.make_async_remote_copy(
            src_ref=edge_src.at[side],
            dst_ref=blocks.at[subs + 1 if side == 0 else 0],
            send_sem=edge_send.at[side], recv_sem=edge_recv.at[side],
            device_id={"mem": other % quarters, "cell": other // quarters},
            device_id_type=MESH,
        )

    @pl.when(place > 0)
    def _():
        edge(0).start()

    @pl.when(place < last_place)
    def _():
        edge(1).start()

    @pl.when(place == 0)
    def _():
        blocks[0] = jnp.zeros((part, LANES), jnp.float32)

    @pl.when(place == last_place)
    def _():
        blocks[subs + 1] = jnp.zeros((part, LANES), jnp.float32)

    for k in range(1, quarters):
        tell_mem(k).wait_recv()
        mine = mine + mem_stats[k]
    cell_src[...] = mine

    def tell_cell(k):
        return pltpu.make_async_remote_copy(
            src_ref=cell_src, dst_ref=cell_stats.at[k],
            send_sem=cs_send.at[k], recv_sem=cs_recv.at[k],
            device_id={"cell": (slab + k) % slabs}, device_id_type=MESH,
        )

    def start_cell(k, _):
        tell_cell(k).start()
        return 0

    for k in range(1, slabs):
        start_cell(k, 0)

    @pl.when(place > 0)
    def _():
        edge(1).wait_recv()

    @pl.when(place < last_place)
    def _():
        edge(0).wait_recv()

    def take_cell(k, total):
        tell_cell(k).wait_recv()
        return total + cell_stats[k]

    total = mine
    for k in range(1, slabs):
        total = take_cell(k, total)
    total = total[:1]
    lane1 = lane[:1]
    misfit = jnp.sum(jnp.where(lane1 == 0, total, 0.0), keepdims=True)
    spread = jnp.sum(jnp.where(lane1 == 1, total, 0.0), keepdims=True)
    rho = jnp.sqrt(misfit / (spread / (members - 1) + total_obs))

    wide = GROUP * members
    wr = lax.broadcasted_iota(jnp.int32, (members, wide), 0)
    wc = lax.broadcasted_iota(jnp.int32, (members, wide), 1)
    eye = jnp.where(wc % members == wr, 1.0, 0.0)
    owner_lane = wc[:1] // members
    sr = lax.broadcasted_iota(jnp.int32, (wide, wide), 0) // members
    sc = lax.broadcasted_iota(jnp.int32, (wide, wide), 1) // members
    own_block = jnp.where(sr == sc, 1.0, 0.0).astype(jnp.bfloat16)

    def spreadout(x):
        return jnp.concatenate([x] * GROUP, axis=0) * own_block

    def times(left, right):
        rh, rl = split(right)
        rh, rl = spreadout(rh), spreadout(rl)
        lh, ll = split(left)
        return dot(lh, rh) + (dot(ll, rh) + dot(lh, rl))

    groups = subs // GROUP
    state = []
    sides = []
    for g in range(groups):
        parts = []
        for p in range(g * GROUP, (g + 1) * GROUP):
            parts.append((blocks[p] + blocks[p + 1] + blocks[p + 2])[:, :members])
        joined = jnp.concatenate(parts, axis=1)
        system = eye + (rho * rho / (members - 1)) * joined[:members]
        squares = jnp.sum(system * system, axis=0, keepdims=True)
        norm = jnp.zeros((1, wide), jnp.float32)
        for p in range(GROUP):
            here = owner_lane == p
            norm = jnp.where(here, jnp.sum(jnp.where(here, squares, 0.0), keepdims=True), norm)
        norm = jnp.sqrt(norm)
        state.append((system / norm, eye))
        sides.append((norm, joined[members:]))

    def newton(_, carry):
        out = []
        for current, invroot in carry:
            factor = 1.5 * eye - 0.5 * times(invroot, current)
            both = times(jnp.concatenate([current, invroot], axis=0), factor)
            out.append((both[:members], both[members:]))
        return tuple(out)

    state = lax.fori_loop(0, NS_ITERS, newton, tuple(state))
    for g in range(groups):
        inverse = state[g][1]
        norm, cross = sides[g]
        solved = times(times(cross, inverse), inverse)[:1] / norm
        mean_weight = rho / (members - 1) * solved
        full = rho * (inverse / jnp.sqrt(norm) + mean_weight)
        high, low = split(full)
        for p in range(GROUP):
            at = slice(p * members, (p + 1) * members)
            mixing[g * GROUP + p] = jnp.concatenate([high[:, at], high[:, at], low[:, at]], axis=1)

    def back(field, sub, k, arriving=False):
        peer = (me + k) % quarters
        owner = (me - k + quarters) % quarters if arriving else me
        source = (an_d, an_f)[field]
        target = (out_depth, out_flow)[field]
        at = pl.multiple_of(sub * PER, PER)
        src_ref = source.at[pl.ds(pl.multiple_of(peer * rows, rows), rows), pl.ds(at, PER)]
        dst_ref = target.at[:, pl.ds(pl.multiple_of(owner * quart + at, PER), PER)]
        return pltpu.make_async_remote_copy(
            src_ref=src_ref, dst_ref=dst_ref,
            send_sem=back_send.at[field, k, sub], recv_sem=back_recv.at[field, k, sub],
            device_id={"mem": peer}, device_id_type=MESH,
        )

    def back_keep(field):
        source = (an_d, an_f)[field]
        target = (out_depth, out_flow)[field]
        return pltpu.make_async_copy(
            source.at[pl.ds(pl.multiple_of(me * rows, rows), rows), :],
            target.at[:, pl.ds(pl.multiple_of(me * quart, quart), quart)],
            back_own.at[field],
        )

    for field in range(2):
        window = (win_d, win_f)[field]
        analysed = (an_d, an_f)[field]
        if field == 1:
            for k in range(1, quarters):
                go(1, k, True).wait_recv()

        def analyse(sub, _):
            at = pl.ds(pl.multiple_of(sub * PER, PER), PER)
            x = window[:, at]
            mean = jnp.mean(x, axis=0, keepdims=True)
            high, low = split(x - mean)
            stacked = jnp.concatenate([high, low, high], axis=0)
            analysed[:, at] = mean + dot(mixing[sub], stacked)
            for k in range(1, quarters):
                back(field, sub, k).start()
            return 0

        for sub in range(subs):
            analyse(sub, 0)
        back_keep(field).start()

    @pl.when(has_high)
    def _():
        for i in range(5):
            halo(0, i).wait_send()

    @pl.when(has_low)
    def _():
        for i in range(5):
            halo(1, i).wait_send()

    @pl.when(place > 0)
    def _():
        edge(0).wait_send()

    @pl.when(place < last_place)
    def _():
        edge(1).wait_send()

    for k in range(1, quarters):
        tell_mem(k).wait_send()
        for field in range(2):
            go(field, k).wait_send()

    def end_cell(k, _):
        tell_cell(k).wait_send()
        return 0

    for k in range(1, slabs):
        end_cell(k, 0)
    for field in range(2):
        back_keep(field).wait()

        def finish(sub, _):
            for k in range(1, quarters):
                back(field, sub, k).wait_send()
                back(field, sub, k, True).wait_recv()
            return 0

        for sub in range(subs):
            finish(sub, 0)


def shards(depth, discharge, gate, pump, pump_rate, obs_index, obs_value, obs_error):
    rows, cells = depth.shape
    slabs = lax.axis_size("cell")
    quarters = lax.axis_size("mem")
    members = rows * quarters
    quart = cells // quarters
    subs = quart // PER
    steps = pump.shape[0]
    padded = cells + 2 * LANES
    part = members + 8
    f32, i32 = jnp.float32, jnp.int32
    dma = pltpu.SemaphoreType.DMA
    scratch = [
        pltpu.VMEM((rows, padded), f32),
        pltpu.VMEM((rows, padded), f32),
        pltpu.VMEM((1, padded), i32),
        pltpu.VMEM((steps, padded), i32),
        pltpu.VMEM((1, padded), f32),
        pltpu.VMEM((rows, cells), f32),
        pltpu.VMEM((rows, cells), f32),
        pltpu.VMEM((members, quart), f32),
        pltpu.VMEM((members, quart), f32),
        pltpu.VMEM((members, quart), f32),
        pltpu.VMEM((members, quart), f32),
        pltpu.VMEM((2 * quart // LANES, LANES), f32),
        pltpu.VMEM((subs + 2, part, LANES), f32),
        pltpu.VMEM((2, part, LANES), f32),
        pltpu.VMEM((8, LANES), f32),
        pltpu.VMEM((quarters, 8, LANES), f32),
        pltpu.VMEM((8, LANES), f32),
        pltpu.VMEM((slabs, 8, LANES), f32),
        pltpu.VMEM((subs, members, 3 * members), jnp.bfloat16),
        dma((5,)),
        dma((2, 5)),
        dma((2, 5)),
        dma((2, quarters)),
        dma((2, quarters)),
        dma((2,)),
        dma((2,)),
        dma((2,)),
        dma((quarters,)),
        dma((quarters,)),
        dma((slabs,)),
        dma((slabs,)),
        dma((2, quarters, subs)),
        dma((2, quarters, subs)),
        dma((2,)),
    ]
    hbm = pl.BlockSpec(memory_space=pl.ANY)
    vmem = pl.BlockSpec(memory_space=pltpu.VMEM)
    return pl.pallas_call(
        functools.partial(kernel, quarters, slabs),
        out_shape=[jax.ShapeDtypeStruct((rows, cells), f32)] * 2,
        in_specs=[hbm] * 5 + [vmem] * 3,
        out_specs=[hbm] * 2,
        scratch_shapes=scratch,
        compiler_params=pltpu.CompilerParams(collective_id=0, has_side_effects=True),
    )(
        depth, discharge, gate.reshape(1, cells), pump, pump_rate.reshape(1, cells),
        obs_index, obs_value, obs_error,
    )


def solution(mesh):
    return jax.shard_map(
        shards,
        mesh=mesh,
        in_specs=(
            P("mem", "cell"),
            P("mem", "cell"),
            P("cell"),
            P(None, "cell"),
            P("cell"),
            P("cell", None),
            P("cell", None),
            P("cell", None),
        ),
        out_specs=(P("mem", "cell"), P("mem", "cell")),
        check_vma=False,
    )
```

```python
import functools

import jax
import jax.numpy as jnp
from jax import lax
from jax.experimental import pallas as pl
from jax.experimental.pallas import tpu as pltpu
from jax.sharding import PartitionSpec as P

PER = 512
NS_ITERS = 12
LANES = 128
CHUNK = 2048
GROUP = 4
MESH = pl.DeviceIdType.MESH

gravity = 9.81
step_dt = 0.06


def rolled(x, shift):
    return pltpu.roll(x, shift % x.shape[1], 1)


def advance(h, q, opened, inflow):
    u = q / h
    c = jnp.sqrt(gravity * h)
    low = u - c
    top = u + c
    still = (0.5 * gravity) * h * h
    moment = q * u + still
    h_left = rolled(h, 1)
    q_left = rolled(q, 1)
    still_left = rolled(still, 1)
    moment_left = rolled(moment, 1)
    a = jnp.minimum(jnp.minimum(rolled(low, 1), low), 0.0)
    b = jnp.maximum(jnp.maximum(rolled(top, 1), top), 0.0)
    inverse = 1.0 / (b - a)
    ab = a * b
    mass = (b * q_left - a * q + ab * (h - h_left)) * inverse
    flux = (b * moment_left - a * moment + ab * (q - q_left)) * inverse
    mass = jnp.where(opened, mass, 0.0)
    left_side = jnp.where(opened, flux, still_left)
    right_side = jnp.where(opened, flux, still)
    h_new = h - step_dt * (rolled(mass, -1) - mass) + step_dt * inflow
    q_new = q - step_dt * (rolled(left_side, -1) - right_side)
    return h_new, q_new


def split(x):
    high = x.astype(jnp.bfloat16)
    return high, (x - high.astype(jnp.float32)).astype(jnp.bfloat16)


def dot(x, y):
    return jnp.dot(x, y, preferred_element_type=jnp.float32)


def dot_t(x, y):
    return lax.dot_general(x, y, (((1,), (1,)), ((), ())), preferred_element_type=jnp.float32)


def kernel(
    quarters, slabs,
    depth, flow, gate, pump, rate, obs_index, obs_value, obs_error,
    out_depth, out_flow,
    d_pad, f_pad, g_pad, p_pad, r_pad, fc_d, fc_f, win_d, win_f, an_d, an_f,
    obs_rows, blocks, edge_src, stats, mem_stats, cell_src, cell_stats, mixing,
    load_sem, halo_send, halo_recv, go_send, go_recv, own_sem,
    edge_send, edge_recv, ms_send, ms_recv, cs_send, cs_recv, back_send, back_recv, back_own,
):
    me = lax.axis_index("mem")
    slab = lax.axis_index("cell")
    rows, cells = depth.shape
    members = rows * quarters
    quart = cells // quarters
    subs = quart // PER
    steps = pump.shape[0]
    total_obs = obs_index.shape[1] * slabs
    pads = (d_pad, f_pad, g_pad, p_pad, r_pad)
    sources = (depth, flow, gate, pump, rate)
    place = slab * quarters + me
    last_place = slabs * quarters - 1
    has_low = slab > 0
    has_high = slab < slabs - 1

    loads = [
        pltpu.make_async_copy(src, pad.at[:, pl.ds(LANES, cells)], load_sem.at[i])
        for i, (src, pad) in enumerate(zip(sources, pads))
    ]
    for copy in loads:
        copy.start()

    barrier = pltpu.get_barrier_semaphore()
    for k in range(1, quarters):
        pl.semaphore_signal(
            barrier, inc=1, device_id={"mem": (me + k) % quarters}, device_id_type=MESH
        )

    def greet(k, _):
        pl.semaphore_signal(barrier, inc=1, device_id={"cell": (slab + k) % slabs}, device_id_type=MESH)
        return 0

    for k in range(1, slabs):
        greet(k, 0)
    cross_low = jnp.logical_and(me == 0, has_low)
    cross_high = jnp.logical_and(me == quarters - 1, has_high)

    @pl.when(cross_low)
    def _():
        pl.semaphore_signal(
            barrier, inc=1, device_id={"mem": quarters - 1, "cell": (slab + slabs - 1) % slabs}, device_id_type=MESH
        )

    @pl.when(cross_high)
    def _():
        pl.semaphore_signal(
            barrier, inc=1, device_id={"mem": 0, "cell": (slab + 1) % slabs}, device_id_type=MESH
        )

    crossing = cross_low.astype(jnp.int32) + cross_high.astype(jnp.int32)
    pl.semaphore_wait(barrier, quarters - 1 + slabs - 1 + crossing)

    def halo(side, i):
        start = cells - LANES if side == 0 else 0
        target = 0 if side == 0 else cells + LANES
        return pltpu.make_async_remote_copy(
            src_ref=sources[i].at[:, pl.ds(start, LANES)],
            dst_ref=pads[i].at[:, pl.ds(target, LANES)],
            send_sem=halo_send.at[side, i],
            recv_sem=halo_recv.at[side, i],
            device_id={"cell": (slab + 1 if side == 0 else slab + slabs - 1) % slabs},
            device_id_type=MESH,
        )

    @pl.when(has_high)
    def _():
        for i in range(5):
            halo(0, i).start()

    @pl.when(has_low)
    def _():
        for i in range(5):
            halo(1, i).start()

    offsets = obs_index[...] - me * quart
    value = obs_value[...]
    precision = 1.0 / obs_error[...]
    coarse = offsets // LANES
    fine = offsets - coarse * LANES
    count = obs_index.shape[1]
    row_count = quart // LANES
    at_row = lax.broadcasted_iota(jnp.int32, (row_count, count), 0) == coarse
    at_lane = (lax.broadcasted_iota(jnp.int32, (LANES, count), 0) == fine).astype(jnp.float32)
    picked = jnp.concatenate(
        [jnp.where(at_row, value, 0.0), jnp.where(at_row, precision, 0.0)], axis=0
    )
    obs_rows[...] = lax.dot_general(
        picked, at_lane, (((1,), (1,)), ((), ())),
        precision=lax.Precision.HIGHEST, preferred_element_type=jnp.float32,
    )

    for copy in loads:
        copy.wait()

    @pl.when(has_low)
    def _():
        for i in range(5):
            halo(0, i).wait_recv()

    @pl.when(has_high)
    def _():
        for i in range(5):
            halo(1, i).wait_recv()

    width = CHUNK + 2 * LANES

    def forecast(chunk):
        start = pl.multiple_of(chunk * CHUNK, CHUNK)
        at = pl.ds(start, width)
        cell = lax.broadcasted_iota(jnp.int32, (1, width), 1) + (slab * cells + start - LANES)
        inside = jnp.logical_and(cell > 0, cell < slabs * cells)
        opened = jnp.logical_and(g_pad[:, at] > 0, inside)
        h = d_pad[:, at]
        q = f_pad[:, at]
        for step in range(steps):
            inflow = r_pad[:, at] * p_pad[step : step + 1, at].astype(jnp.float32)
            h, q = advance(h, q, opened, inflow)
        fc_d[:, pl.ds(start, CHUNK)] = h[:, LANES : LANES + CHUNK]
        fc_f[:, pl.ds(start, CHUNK)] = q[:, LANES : LANES + CHUNK]

    per_quart = quart // CHUNK

    def go(field, k, arriving=False):
        peer = (me + k) % quarters
        owner = (me - k + quarters) % quarters if arriving else me
        source = (fc_d, fc_f)[field]
        target = (win_d, win_f)[field]
        return pltpu.make_async_remote_copy(
            src_ref=source.at[:, pl.ds(pl.multiple_of(peer * quart, quart), quart)],
            dst_ref=target.at[pl.ds(pl.multiple_of(owner * rows, rows), rows), :],
            send_sem=go_send.at[field, k],
            recv_sem=go_recv.at[field, k],
            device_id={"mem": peer},
            device_id_type=MESH,
        )

    def keep(field):
        source = (fc_d, fc_f)[field]
        target = (win_d, win_f)[field]
        return pltpu.make_async_copy(
            source.at[:, pl.ds(pl.multiple_of(me * quart, quart), quart)],
            target.at[pl.ds(pl.multiple_of(me * rows, rows), rows), :],
            own_sem.at[field],
        )

    for k in range(1, quarters + 1):
        peer = (me + k) % quarters

        def one(j, _):
            forecast(peer * per_quart + j)
            return 0

        lax.fori_loop(0, per_quart, one, 0)
        if k < quarters:
            go(0, k).start()
        else:
            keep(0).start()
            keep(1).start()
    for k in range(1, quarters):
        go(1, k).start()

    keep(0).wait()
    keep(1).wait()
    for k in range(1, quarters):
        go(0, k, True).wait_recv()

    pieces = PER // LANES
    extra = 8
    first_extra = lax.broadcasted_iota(jnp.int32, (extra, PER), 0) == 0

    def obs_of(sub, base):
        first_row = base + sub * pieces
        at = [obs_rows[first_row + i : first_row + i + 1, :] for i in range(pieces)]
        return jnp.concatenate(at, axis=1)

    def gram(sub, total):
        x = win_d[:, sub * PER : (sub + 1) * PER]
        mean = jnp.mean(x, axis=0, keepdims=True)
        weight = obs_of(sub, row_count)
        scaled = (x - mean) * weight
        innov = (obs_of(sub, 0) - mean) * weight
        tall = jnp.concatenate(
            [
                scaled,
                jnp.where(first_extra, innov, 0.0),
                jnp.zeros((LANES - members - extra, PER), jnp.float32),
            ],
            axis=0,
        )
        high, low = split(tall)
        part = members + extra
        both = jnp.concatenate([high[:80], low[:80]], axis=0)
        first = dot_t(both, high)
        block = first[:part] + first[80 : 80 + part] + dot_t(high[:80], low)[:part]
        blocks[sub + 1] = block
        return total + block

    part = members + extra
    summed = jnp.zeros((part, LANES), jnp.float32)
    for sub in range(subs):
        summed = gram(sub, summed)
    ri = lax.broadcasted_iota(jnp.int32, (part, LANES), 0)
    ci = lax.broadcasted_iota(jnp.int32, (part, LANES), 1)
    diagonal = jnp.where(ri == ci, summed, 0.0)
    spread = jnp.sum(jnp.where(ri < members, diagonal, 0.0), keepdims=True)
    misfit = jnp.sum(jnp.where(ri == members, diagonal, 0.0), keepdims=True)
    lane = lax.broadcasted_iota(jnp.int32, (8, LANES), 1)
    mine = jnp.where(lane == 0, misfit, jnp.where(lane == 1, spread, 0.0))
    stats[...] = mine
    edge_src[0] = blocks[1]
    edge_src[1] = blocks[subs]

    def tell_mem(k):
        return pltpu.make_async_remote_copy(
            src_ref=stats, dst_ref=mem_stats.at[k],
            send_sem=ms_send.at[k], recv_sem=ms_recv.at[k],
            device_id={"mem": (me + k) % quarters}, device_id_type=MESH,
        )

    for k in range(1, quarters):
        tell_mem(k).start()

    def edge(side):
        other = (place + last_place if side == 0 else place + 1) % (last_place + 1)
        return pltpu.make_async_remote_copy(
            src_ref=edge_src.at[side],
            dst_ref=blocks.at[subs + 1 if side == 0 else 0],
            send_sem=edge_send.at[side], recv_sem=edge_recv.at[side],
            device_id={"mem": other % quarters, "cell": other // quarters},
            device_id_type=MESH,
        )

    @pl.when(place > 0)
    def _():
        edge(0).start()

    @pl.when(place < last_place)
    def _():
        edge(1).start()

    @pl.when(place == 0)
    def _():
        blocks[0] = jnp.zeros((part, LANES), jnp.float32)

    @pl.when(place == last_place)
    def _():
        blocks[subs + 1] = jnp.zeros((part, LANES), jnp.float32)

    for k in range(1, quarters):
        tell_mem(k).wait_recv()
        mine = mine + mem_stats[k]
    cell_src[...] = mine

    def tell_cell(k):
        return pltpu.make_async_remote_copy(
            src_ref=cell_src, dst_ref=cell_stats.at[k],
            send_sem=cs_send.at[k], recv_sem=cs_recv.at[k],
            device_id={"cell": (slab + k) % slabs}, device_id_type=MESH,
        )

    def start_cell(k, _):
        tell_cell(k).start()
        return 0

    for k in range(1, slabs):
        start_cell(k, 0)

    @pl.when(place > 0)
    def _():
        edge(1).wait_recv()

    @pl.when(place < last_place)
    def _():
        edge(0).wait_recv()

    def take_cell(k, total):
        tell_cell(k).wait_recv()
        return total + cell_stats[k]

    total = mine
    for k in range(1, slabs):
        total = take_cell(k, total)
    total = total[:1]
    lane1 = lane[:1]
    misfit = jnp.sum(jnp.where(lane1 == 0, total, 0.0), keepdims=True)
    spread = jnp.sum(jnp.where(lane1 == 1, total, 0.0), keepdims=True)
    rho = jnp.sqrt(misfit / (spread / (members - 1) + total_obs))

    wide = GROUP * members
    wr = lax.broadcasted_iota(jnp.int32, (members, wide), 0)
    wc = lax.broadcasted_iota(jnp.int32, (members, wide), 1)
    eye = jnp.where(wc % members == wr, 1.0, 0.0)
    owner_lane = wc[:1] // members
    sr = lax.broadcasted_iota(jnp.int32, (wide, wide), 0) // members
    sc = lax.broadcasted_iota(jnp.int32, (wide, wide), 1) // members
    own_block = jnp.where(sr == sc, 1.0, 0.0).astype(jnp.bfloat16)

    def spreadout(x):
        return jnp.concatenate([x] * GROUP, axis=0) * own_block

    def times(left, right):
        rh, rl = split(right)
        rh, rl = spreadout(rh), spreadout(rl)
        lh, ll = split(left)
        return dot(lh, rh) + (dot(ll, rh) + dot(lh, rl))

    groups = subs // GROUP
    state = []
    sides = []
    for g in range(groups):
        parts = []
        for p in range(g * GROUP, (g + 1) * GROUP):
            parts.append((blocks[p] + blocks[p + 1] + blocks[p + 2])[:, :members])
        joined = jnp.concatenate(parts, axis=1)
        system = eye + (rho * rho / (members - 1)) * joined[:members]
        squares = jnp.sum(system * system, axis=0, keepdims=True)
        norm = jnp.zeros((1, wide), jnp.float32)
        for p in range(GROUP):
            here = owner_lane == p
            norm = jnp.where(here, jnp.sum(jnp.where(here, squares, 0.0), keepdims=True), norm)
        norm = jnp.sqrt(norm)
        state.append((system / norm, eye))
        sides.append((norm, joined[members:]))

    def newton(_, carry):
        out = []
        for current, invroot in carry:
            factor = 1.5 * eye - 0.5 * times(invroot, current)
            both = times(jnp.concatenate([current, invroot], axis=0), factor)
            out.append((both[:members], both[members:]))
        return tuple(out)

    state = lax.fori_loop(0, NS_ITERS, newton, tuple(state))
    for g in range(groups):
        inverse = state[g][1]
        norm, cross = sides[g]
        solved = times(times(cross, inverse), inverse)[:1] / norm
        mean_weight = rho / (members - 1) * solved
        full = rho * (inverse / jnp.sqrt(norm) + mean_weight)
        high, low = split(full)
        for p in range(GROUP):
            at = slice(p * members, (p + 1) * members)
            mixing[g * GROUP + p] = jnp.concatenate([high[:, at], high[:, at], low[:, at]], axis=1)

    def back(field, sub, k, arriving=False):
        peer = (me + k) % quarters
        owner = (me - k + quarters) % quarters if arriving else me
        source = (an_d, an_f)[field]
        target = (out_depth, out_flow)[field]
        at = pl.multiple_of(sub * PER, PER)
        src_ref = source.at[pl.ds(pl.multiple_of(peer * rows, rows), rows), pl.ds(at, PER)]
        dst_ref = target.at[:, pl.ds(pl.multiple_of(owner * quart + at, PER), PER)]
        return pltpu.make_async_remote_copy(
            src_ref=src_ref, dst_ref=dst_ref,
            send_sem=back_send.at[field, k, sub], recv_sem=back_recv.at[field, k, sub],
            device_id={"mem": peer}, device_id_type=MESH,
        )

    def back_keep(field):
        source = (an_d, an_f)[field]
        target = (out_depth, out_flow)[field]
        return pltpu.make_async_copy(
            source.at[pl.ds(pl.multiple_of(me * rows, rows), rows), :],
            target.at[:, pl.ds(pl.multiple_of(me * quart, quart), quart)],
            back_own.at[field],
        )

    for field in range(2):
        window = (win_d, win_f)[field]
        analysed = (an_d, an_f)[field]
        if field == 1:
            for k in range(1, quarters):
                go(1, k, True).wait_recv()

        def analyse(sub, _):
            at = pl.ds(pl.multiple_of(sub * PER, PER), PER)
            x = window[:, at]
            mean = jnp.mean(x, axis=0, keepdims=True)
            high, low = split(x - mean)
            stacked = jnp.concatenate([high, low, high], axis=0)
            analysed[:, at] = mean + dot(mixing[sub], stacked)
            for k in range(1, quarters):
                back(field, sub, k).start()
            return 0

        for sub in range(subs):
            analyse(sub, 0)
        back_keep(field).start()

    @pl.when(has_high)
    def _():
        for i in range(5):
            halo(0, i).wait_send()

    @pl.when(has_low)
    def _():
        for i in range(5):
            halo(1, i).wait_send()

    @pl.when(place > 0)
    def _():
        edge(0).wait_send()

    @pl.when(place < last_place)
    def _():
        edge(1).wait_send()

    for k in range(1, quarters):
        tell_mem(k).wait_send()
        for field in range(2):
            go(field, k).wait_send()

    def end_cell(k, _):
        tell_cell(k).wait_send()
        return 0

    for k in range(1, slabs):
        end_cell(k, 0)
    for field in range(2):
        back_keep(field).wait()

        def finish(sub, _):
            for k in range(1, quarters):
                back(field, sub, k).wait_send()
                back(field, sub, k, True).wait_recv()
            return 0

        for sub in range(subs):
            finish(sub, 0)


def shards(depth, discharge, gate, pump, pump_rate, obs_index, obs_value, obs_error):
    rows, cells = depth.shape
    slabs = lax.axis_size("cell")
    quarters = lax.axis_size("mem")
    members = rows * quarters
    quart = cells // quarters
    subs = quart // PER
    steps = pump.shape[0]
    padded = cells + 2 * LANES
    part = members + 8
    f32, i32 = jnp.float32, jnp.int32
    dma = pltpu.SemaphoreType.DMA
    scratch = [
        pltpu.VMEM((rows, padded), f32),
        pltpu.VMEM((rows, padded), f32),
        pltpu.VMEM((1, padded), i32),
        pltpu.VMEM((steps, padded), i32),
        pltpu.VMEM((1, padded), f32),
        pltpu.VMEM((rows, cells), f32),
        pltpu.VMEM((rows, cells), f32),
        pltpu.VMEM((members, quart), f32),
        pltpu.VMEM((members, quart), f32),
        pltpu.VMEM((members, quart), f32),
        pltpu.VMEM((members, quart), f32),
        pltpu.VMEM((2 * quart // LANES, LANES), f32),
        pltpu.VMEM((subs + 2, part, LANES), f32),
        pltpu.VMEM((2, part, LANES), f32),
        pltpu.VMEM((8, LANES), f32),
        pltpu.VMEM((quarters, 8, LANES), f32),
        pltpu.VMEM((8, LANES), f32),
        pltpu.VMEM((slabs, 8, LANES), f32),
        pltpu.VMEM((subs, members, 3 * members), jnp.bfloat16),
        dma((5,)),
        dma((2, 5)),
        dma((2, 5)),
        dma((2, quarters)),
        dma((2, quarters)),
        dma((2,)),
        dma((2,)),
        dma((2,)),
        dma((quarters,)),
        dma((quarters,)),
        dma((slabs,)),
        dma((slabs,)),
        dma((2, quarters, subs)),
        dma((2, quarters, subs)),
        dma((2,)),
    ]
    hbm = pl.BlockSpec(memory_space=pl.ANY)
    vmem = pl.BlockSpec(memory_space=pltpu.VMEM)
    return pl.pallas_call(
        functools.partial(kernel, quarters, slabs),
        out_shape=[jax.ShapeDtypeStruct((rows, cells), f32)] * 2,
        in_specs=[hbm] * 5 + [vmem] * 3,
        out_specs=[hbm] * 2,
        scratch_shapes=scratch,
        compiler_params=pltpu.CompilerParams(collective_id=0, has_side_effects=True),
    )(
        depth, discharge, gate.reshape(1, cells), pump, pump_rate.reshape(1, cells),
        obs_index, obs_value, obs_error,
    )


def solution(mesh):
    return jax.shard_map(
        shards,
        mesh=mesh,
        in_specs=(
            P("mem", "cell"),
            P("mem", "cell"),
            P("cell"),
            P(None, "cell"),
            P("cell"),
            P("cell", None),
            P("cell", None),
            P("cell", None),
        ),
        out_specs=(P("mem", "cell"), P("mem", "cell")),
        check_vma=False,
    )
```
